32 devices in a mesh: groups: 2 (over y), pipe: 8 (over z, x), tensor: 2 (over core).
Axes of the slice: x: 2, y: 2, z: 4, core: 2. Of those that a mesh axis runs over, the one named last changes fastest.
Arguments:
- hidden: bfloat16 [2, 16, 8192], P(None, ('groups', 'pipe'), 'tensor'), parts along dimension 1, may hold values from -16 to 16
- labels: int32 [2, 16], P(None, 'groups'), parts along dimension 1, may hold values from 0 to 4095
- upstream: float32 [2, 16], P(None, 'groups'), parts along dimension 1, may hold values from 16 to 48
- out_weight: bfloat16 [8192, 8192], P(('groups', 'pipe'), 'tensor'), parts along dimension 0
Outputs:
- loss: float32 [2, 16], P(None, ('groups', 'pipe')), parts along dimension 1
- hidden_grad: bfloat16 [2, 16, 8192], P(None, ('groups', 'pipe'), 'tensor'), parts along dimension 1
The draws below stay inside these ranges and needn't reach their ends.
There are 2 independent parts, one for each index of `groups`. The reference program is written for one: setup_inputs(seed, part) draws one part's arguments, and reference() takes and returns one part's arrays. A program takes and returns all parts, laid end to end along the dimension named above; each array names one. Nothing has to cross between parts.
All inputs are finite; a program needn't handle non-finite values.
Results may differ from the reference program's by a relative error of at most 0.0047.
Values may be sent and summed in bfloat16 or wider, within the bound.
A program may use at most 64 MiB of HBM per device.

```python
import math
import jax
import jax.numpy as jnp
import numpy as np
from jax import lax

D = 8192
MB = 2
TOK = 8
VOCAB = 4096


def base_weight(key):
    drawn = jax.random.normal(jax.random.fold_in(key, 11), (VOCAB, D), jnp.float32)
    return jnp.clip(drawn, -6.0, 6.0) * (3.0 / math.sqrt(D))


def draw_out_weight(key, part):
    return base_weight(key).astype(jnp.bfloat16)


def draw_hidden(key, part):
    drawn = jnp.clip(jax.random.normal(jax.random.fold_in(key, 23), (MB, TOK, D), jnp.float32), -6.0, 6.0)
    return drawn.astype(jnp.bfloat16)


def touch_ends(array, key, least, largest):
    longest = array.shape.index(max(array.shape))
    spots = []
    for shift in (0, 1):
        where = [jax.random.randint(jax.random.fold_in(key, axis), (), 0, length) for axis, length in enumerate(array.shape)]
        where[longest] = (where[longest] + shift) % array.shape[longest]
        spots.append(tuple(where))
    return array.at[spots[0]].set(least).at[spots[1]].set(largest)


def rank_table(number_of, skew):
    portions = [(1 << 20) // math.isqrt(standing ** skew) + 1 for standing in range(1, number_of + 1)]
    deviation = 1 + sum(portions) // (1 << 30)
    return np.cumsum(np.array([max(1, weight // deviation) for weight in portions]))


def ranked(stream_key, extent, number_of, skew):
    listing = rank_table(number_of, skew)
    ticket = jax.random.randint(jax.random.fold_in(stream_key, 1), extent, 0, int(listing[number_of - 1]))
    rank = jnp.searchsorted(jnp.asarray(listing, jnp.int32), ticket, side="right")
    return jax.random.permutation(jax.random.fold_in(stream_key, 2), number_of)[rank].astype(jnp.int32)


def setup_inputs(seed: int = 0, part: int = 0) -> dict:
    splits = jax.random.split(jax.random.key(seed), 5)
    part_splits = jax.random.split(jax.random.fold_in(splits[4], part), 5)
    return {
        "hidden": draw_hidden(jax.random.fold_in(jax.random.fold_in(splits[4], part), 71), part),
        "labels": touch_ends(ranked(part_splits[1], (MB, TOK), VOCAB, 2), jax.random.fold_in(part_splits[1], 3), 0, VOCAB - 1).astype(jnp.int32),
        "upstream": jnp.clip(jax.random.uniform(part_splits[2], (MB, TOK), jnp.float32, 16.0, 48.0), 16.0, 48.0),
        "out_weight": draw_out_weight(jax.random.fold_in(jax.random.fold_in(splits[4], part), 71), part),
    }


def reference(hidden, labels, upstream, out_weight):
    loss_list = []
    grad_list = []
    vocab_ids = lax.broadcasted_iota(jnp.int32, (1, out_weight.shape[0]), 1)
    for micro in range(hidden.shape[0]):
        logits = lax.dot_general(hidden[micro], out_weight, (((1,), (1,)), ((), ())), preferred_element_type=jnp.float32)
        row_max = jnp.max(logits, axis=1)
        row_total = jnp.sum(jnp.exp(logits - row_max[:, None]), axis=1)
        onehot = (labels[micro][:, None] == vocab_ids).astype(jnp.float32)
        target = jnp.sum(logits * onehot, axis=1)
        log_total = row_max + jnp.log(row_total)
        loss_list.append(log_total - target)
        probs = jnp.exp(logits - log_total[:, None])
        grad_logits = (upstream[micro][:, None] * (probs - onehot)).astype(jnp.bfloat16)
        grad_list.append(jnp.dot(grad_logits, out_weight, preferred_element_type=jnp.float32).astype(jnp.bfloat16))
    return jnp.stack(loss_list), jnp.stack(grad_list)
```

```python
import functools

import jax
import jax.numpy as jnp
from jax import lax
from jax.experimental import pallas as pl
from jax.experimental.pallas import tpu as pltpu
from jax.sharding import PartitionSpec as P

F32 = jnp.float32
BF16 = jnp.bfloat16
UNROLL = 16


def each(count, body):
    if count <= UNROLL:
        for i in range(count):
            body(i)
    else:

        @pl.loop(0, count)
        def _(i):
            body(i)


def kernel(
    n,
    mb,
    chunks,
    h_hbm,
    lab_hbm,
    up_hbm,
    w_hbm,
    loss_ref,
    grad_ref,
    w,
    hg,
    rows,
    pl_send,
    pl_recv,
    st,
    b_out,
    b_in,
    g_out,
    g_in,
    lab_ref,
    up_ref,
    w_sem,
    in_sem,
    h_send,
    h_recv,
    l_send,
    l_recv,
    b_send,
    b_recv,
    s_send,
    s_recv,
    g_send,
    g_recv,
):
    me = lax.axis_index("pipe")
    core = lax.axis_index("tensor")
    voc, width = w_hbm.shape
    tokens = n * mb
    vc = voc // chunks

    def w_copy(c):
        part = pl.ds(c * vc, vc)
        return pltpu.make_async_copy(w_hbm.at[part], w.at[part], w_sem.at[c])

    barrier = pltpu.get_barrier_semaphore()
    pl.semaphore_signal(barrier, inc=1, device_id={"tensor": 1 - core})

    def others(body, last_first=False):
        def one(i):
            q = n - 1 - i if last_first else i

            @pl.when(q != me)
            def _():
                body(q)

        each(n, one)

    others(lambda q: pl.semaphore_signal(barrier, inc=1, device_id={"pipe": q}))

    inputs = (
        pltpu.make_async_copy(h_hbm, hg.at[me], in_sem.at[0]),
        pltpu.make_async_copy(lab_hbm, lab_ref, in_sem.at[1]),
        pltpu.make_async_copy(up_hbm, up_ref, in_sem.at[2]),
    )
    for copy in inputs:
        copy.start()
    for c in range(chunks):
        w_copy(c).start()
    for copy in inputs:
        copy.wait()

    row_f = lax.broadcasted_iota(jnp.int32, (tokens, 1), 0)
    row_tok = row_f // mb
    row_mb = row_f - row_tok * mb
    tok_cols = lax.broadcasted_iota(jnp.int32, (tokens, n), 1)
    label_of = jnp.zeros((tokens, n), F32)
    for m in range(mb):
        label_of = jnp.where(
            (row_mb == m) & (row_tok == tok_cols), lab_ref[m : m + 1, :].astype(F32), label_of
        )
    labels = jnp.sum(label_of, axis=1, keepdims=True).astype(jnp.int32) - me * voc
    hot = labels == lax.broadcasted_iota(jnp.int32, (tokens, voc), 1)

    def pack(p, ref):
        ref[p] = rows[pl.ds(p * mb, mb), :].astype(BF16)

    def product(left):
        step = 1024 if width % 1024 == 0 else width
        for k in range(width // step):
            cols = slice(k * step, (k + 1) * step)
            rows[:, cols] = jnp.dot(left, w[:, cols], preferred_element_type=F32)

    pl.semaphore_wait(barrier, n)

    def h_copy(to):
        return pltpu.make_async_remote_copy(
            src_ref=hg.at[me],
            dst_ref=hg.at[me],
            send_sem=h_send.at[to],
            recv_sem=h_recv.at[me],
            device_id={"pipe": to},
        )

    def h_arrived(source):
        return pltpu.make_async_remote_copy(
            src_ref=hg.at[source],
            dst_ref=hg.at[source],
            send_sem=h_send.at[source],
            recv_sem=h_recv.at[source],
            device_id={"pipe": source},
        )

    others(lambda q: h_copy(q).start(), last_first=True)

    for c in range(chunks):
        w_copy(c).wait()
    product(hot.astype(F32).astype(BF16))
    for p in range(n):
        pack(p, b_out)

    def to_owners(out, into, send, recv):
        def copy(to):
            return pltpu.make_async_remote_copy(
                src_ref=out.at[to],
                dst_ref=into.at[me],
                send_sem=send.at[to],
                recv_sem=recv.at[me],
                device_id={"pipe": to},
            )

        def arrived(source):
            return pltpu.make_async_remote_copy(
                src_ref=out.at[source],
                dst_ref=into.at[source],
                send_sem=send.at[source],
                recv_sem=recv.at[source],
                device_id={"pipe": source},
            )

        return copy, arrived

    b_copy, b_arrived = to_owners(b_out, b_in, b_send, b_recv)
    others(lambda q: h_arrived(q).wait_recv())

    others(lambda q: b_copy(q).start())

    def place(p):
        rows[pl.ds(p * mb, mb), :] = hg[p].astype(F32)

    for p in range(n):
        place(p)
    hidden = rows[...].astype(BF16)

    def l_copy(c):
        return pltpu.make_async_remote_copy(
            src_ref=pl_send.at[c],
            dst_ref=pl_recv.at[c],
            send_sem=l_send.at[c],
            recv_sem=l_recv.at[c],
            device_id={"tensor": 1 - core},
        )

    for c in range(chunks):
        pl_send[c] = lax.dot_general(
            hidden,
            w[c * vc : (c + 1) * vc, :],
            (((1,), (1,)), ((), ())),
            preferred_element_type=F32,
        )
        l_copy(c).start()
    parts = []
    for c in range(chunks):
        l_copy(c).wait_recv()
        parts.append(pl_send[c] + pl_recv[c])
    logits = jnp.concatenate(parts, axis=1)

    top = jnp.max(logits, axis=1, keepdims=True)
    exps = jnp.exp(logits - top)
    total = jnp.sum(exps, axis=1, keepdims=True)
    aim = jnp.sum(jnp.where(hot, logits, 0.0), axis=1, keepdims=True)
    lanes = st.shape[2]
    diag = lax.broadcasted_iota(jnp.int32, (tokens, lanes), 1) == row_f

    def to_lanes(column):
        return jnp.sum(jnp.where(diag, column, 0.0), axis=0, keepdims=True)

    st[me] = jnp.concatenate([to_lanes(top), to_lanes(total), to_lanes(aim), to_lanes(aim)], axis=0)

    def s_copy(to):
        return pltpu.make_async_remote_copy(
            src_ref=st.at[me],
            dst_ref=st.at[me],
            send_sem=s_send.at[to],
            recv_sem=s_recv.at[me],
            device_id={"pipe": to},
        )

    def s_arrived(source):
        return pltpu.make_async_remote_copy(
            src_ref=st.at[source],
            dst_ref=st.at[source],
            send_sem=s_send.at[source],
            recv_sem=s_recv.at[source],
            device_id={"pipe": source},
        )

    others(lambda q: s_copy(q).start())

    product(jnp.where(hot, 0.0, exps).astype(BF16))
    for p in range(n):
        pack(p, g_out)
    g_copy, g_arrived = to_owners(g_out, g_in, g_send, g_recv)
    others(lambda q: g_copy(q).start())

    b_in[me] = b_out[me]
    g_in[me] = g_out[me]
    others(lambda q: b_arrived(q).wait_recv())
    label_row = b_in[0].astype(F32)
    for d in range(1, n):
        label_row += b_in[d].astype(F32)

    others(lambda q: s_arrived(q).wait_recv())
    lane = lax.broadcasted_iota(jnp.int32, (1, lanes), 1)
    spread = []
    pull = []
    for m in range(mb):
        mine = lane == me * mb + m

        def of_token(i):
            return jnp.sum(jnp.where(mine, st[:, i, :], 0.0), axis=1, keepdims=True)

        tops = of_token(0)
        row_max = jnp.max(tops, axis=0, keepdims=True)
        row_total = jnp.sum(of_token(1) * jnp.exp(tops - row_max), axis=0, keepdims=True)
        target = jnp.sum(of_token(2), axis=0, keepdims=True)
        log_total = row_max + jnp.log(row_total)
        loss_ref[:, m : m + 1] = log_total - target
        upstream = jnp.sum(
            jnp.where(
                lax.broadcasted_iota(jnp.int32, (1, n), 1) == me, up_ref[m : m + 1, :], 0.0
            ),
            axis=1,
            keepdims=True,
        )
        spread.append(upstream * jnp.exp(tops - log_total))
        pull.append(
            (upstream * (jnp.exp(target - log_total) - 1.0)).astype(BF16).astype(F32)
        )
    sums = jnp.concatenate(pull, axis=0) * label_row
    for d in range(n):
        @pl.when(d != me)
        def _():
            g_arrived(d).wait_recv()

        scale = jnp.concatenate([spread[m][d : d + 1, :] for m in range(mb)], axis=0)
        sums += scale * g_in[d].astype(F32)
    grad_ref[...] = sums.astype(BF16)

    others(lambda q: h_copy(q).wait_send())
    for c in range(chunks):
        l_copy(c).wait_send()
    others(lambda q: b_copy(q).wait_send())
    others(lambda q: s_copy(q).wait_send())
    others(lambda q: g_copy(q).wait_send())


def hand_over(loss_ref, grad_ref, loss_out, grad_out):
    loss_out[...] = loss_ref[...]
    grad_out[...] = grad_ref[...]


def on_device(n, hidden, labels, upstream, out_weight):
    mb, tok_dev, width = hidden.shape
    voc = out_weight.shape[0]
    tokens = n * mb
    chunks = 1
    lanes = -(-tokens // 128) * 128
    dma = pltpu.SemaphoreType.DMA
    vmem = pl.BlockSpec(memory_space=pltpu.VMEM)
    loss, grad = pl.pallas_call(
        functools.partial(kernel, n, mb, chunks),
        out_shape=(
            pltpu.VMEM((1, mb), F32),
            pltpu.VMEM((mb, width), BF16),
        ),
        in_specs=[pl.BlockSpec(memory_space=pltpu.HBM)] * 4,
        out_specs=(vmem, vmem),
        scratch_shapes=[
            pltpu.VMEM((voc, width), BF16),
            pltpu.VMEM((n, mb, width), BF16),
            pltpu.VMEM((tokens, width), F32),
            pltpu.VMEM((chunks, tokens, voc // chunks), F32),
            pltpu.VMEM((chunks, tokens, voc // chunks), F32),
            pltpu.VMEM((n, 4, lanes), F32),
            pltpu.VMEM((n, mb, width), BF16),
            pltpu.VMEM((n, mb, width), BF16),
            pltpu.VMEM((n, mb, width), BF16),
            pltpu.VMEM((n, mb, width), BF16),
            pltpu.VMEM(labels.shape, labels.dtype),
            pltpu.VMEM(upstream.shape, upstream.dtype),
            dma((chunks,)),
            dma((3,)),
            dma((n,)),
            dma((n,)),
            dma((chunks,)),
            dma((chunks,)),
            dma((n,)),
            dma((n,)),
            dma((n,)),
            dma((n,)),
            dma((n,)),
            dma((n,)),
        ],
        compiler_params=pltpu.CompilerParams(
            collective_id=0, has_side_effects=True, vmem_limit_bytes=56 * 1024 * 1024
        ),
    )(hidden.reshape(mb, width), labels, upstream, out_weight)
    loss = pltpu.with_memory_space_constraint(loss, pltpu.VMEM)
    grad = pltpu.with_memory_space_constraint(grad, pltpu.VMEM)
    loss, grad = pl.pallas_call(
        hand_over,
        out_shape=(
            jax.ShapeDtypeStruct(loss.shape, loss.dtype),
            jax.ShapeDtypeStruct(grad.shape, grad.dtype),
        ),
        in_specs=[vmem, vmem],
        out_specs=(vmem, vmem),
    )(loss, grad)
    return loss.reshape(mb, tok_dev), grad.reshape(mb, tok_dev, width)


def solution(mesh):
    in_specs = (
        P(None, ("groups", "pipe"), "tensor"),
        P(None, "groups"),
        P(None, "groups"),
        P(("groups", "pipe"), "tensor"),
    )
    out_specs = (P(None, ("groups", "pipe")), P(None, ("groups", "pipe"), "tensor"))
    return jax.shard_map(
        functools.partial(on_device, mesh.shape["pipe"]),
        mesh=mesh,
        in_specs=in_specs,
        out_specs=out_specs,
        check_vma=False,
    )
```

```python
import functools

import jax
import jax.numpy as jnp
from jax import lax
from jax.experimental import pallas as pl
from jax.experimental.pallas import tpu as pltpu
from jax.sharding import PartitionSpec as P

F32 = jnp.float32
BF16 = jnp.bfloat16
UNROLL = 16


def each(count, body):
    if count <= UNROLL:
        for i in range(count):
            body(i)
    else:

        @pl.loop(0, count)
        def _(i):
            body(i)


def kernel(
    n,
    mb,
    chunks,
    h_hbm,
    lab_hbm,
    up_hbm,
    w_hbm,
    loss_ref,
    grad_ref,
    w,
    wt,
    hg,
    pl_send,
    pl_recv,
    st,
    b_out,
    b_in,
    g_out,
    g_in,
    lab_ref,
    up_ref,
    w_sem,
    in_sem,
    h_send,
    h_recv,
    l_send,
    l_recv,
    b_send,
    b_recv,
    s_send,
    s_recv,
    g_send,
    g_recv,
):
    me = lax.axis_index("pipe")
    core = lax.axis_index("tensor")
    voc, width = w_hbm.shape
    tokens = n * mb
    wc = width // chunks

    def other(i):
        return jnp.where(me <= i, i + 1, i)

    def others(body):
        each(n - 1, lambda i: body(other(i)))

    def far_first(body):
        each(n - 1, lambda i: body(me ^ (n - 1 - i) if n & (n - 1) == 0 else lax.rem(me + 1 + i, n)))

    def others_back(body):
        each(n - 1, lambda i: body(other(n - 2 - i)))

    barrier = pltpu.get_barrier_semaphore()
    others(lambda q: pl.semaphore_signal(barrier, inc=1, device_id={"pipe": q}))
    pl.semaphore_signal(barrier, inc=1, device_id={"tensor": 1 - core})

    def w_copy(c):
        part = pl.ds(c * wc, wc)
        return pltpu.make_async_copy(w_hbm.at[:, part], w.at[:, part], w_sem.at[c])

    inputs = (
        pltpu.make_async_copy(h_hbm, hg.at[me], in_sem.at[0]),
        pltpu.make_async_copy(lab_hbm, lab_ref, in_sem.at[1]),
        pltpu.make_async_copy(up_hbm, up_ref, in_sem.at[2]),
    )
    for copy in inputs:
        copy.start()
    for c in range(chunks):
        w_copy(c).start()
    for copy in inputs:
        copy.wait()

    row_f = lax.broadcasted_iota(jnp.int32, (tokens, 1), 0)
    row_tok = row_f // mb
    row_mb = row_f - row_tok * mb
    tok_cols = lax.broadcasted_iota(jnp.int32, (tokens, n), 1)
    label_of = jnp.zeros((tokens, n), F32)
    for m in range(mb):
        label_of = jnp.where(
            (row_mb == m) & (row_tok == tok_cols), lab_ref[m : m + 1, :].astype(F32), label_of
        )
    labels = jnp.sum(label_of, axis=1, keepdims=True).astype(jnp.int32) - me * voc
    hot = labels == lax.broadcasted_iota(jnp.int32, (tokens, voc), 1)

    pl.semaphore_wait(barrier, n)

    def to_all(ref, send, recv):
        def copy(to):
            return pltpu.make_async_remote_copy(
                src_ref=ref.at[me],
                dst_ref=ref.at[me],
                send_sem=send.at[to],
                recv_sem=recv.at[me],
                device_id={"pipe": to},
            )

        def arrived(source):
            return pltpu.make_async_remote_copy(
                src_ref=ref.at[source],
                dst_ref=ref.at[source],
                send_sem=send.at[source],
                recv_sem=recv.at[source],
                device_id={"pipe": source},
            )

        return copy, arrived

    def to_owners(out, into, send, recv):
        def copy(to):
            return pltpu.make_async_remote_copy(
                src_ref=out.at[to],
                dst_ref=into.at[me],
                send_sem=send.at[to],
                recv_sem=recv.at[me],
                device_id={"pipe": to},
            )

        def arrived(source):
            return pltpu.make_async_remote_copy(
                src_ref=out.at[source],
                dst_ref=into.at[source],
                send_sem=send.at[source],
                recv_sem=recv.at[source],
                device_id={"pipe": source},
            )

        return copy, arrived

    h_copy, h_arrived = to_all(hg, h_send, h_recv)
    b_copy, b_arrived = to_owners(b_out, b_in, b_send, b_recv)
    s_copy, s_arrived = to_all(st, s_send, s_recv)
    g_copy, g_arrived = to_owners(g_out, g_in, g_send, g_recv)
    l_copy = pltpu.make_async_remote_copy(
        src_ref=pl_send,
        dst_ref=pl_recv,
        send_sem=l_send,
        recv_sem=l_recv,
        device_id={"tensor": 1 - core},
    )

    far_first(lambda q: h_copy(q).start())

    hot_rows = hot.astype(F32).astype(BF16)
    for c in range(chunks):
        w_copy(c).wait()
        cols = slice(c * wc, (c + 1) * wc)
        wt[cols, :] = w[:, cols].T
        label_rows = jnp.dot(hot_rows, w[:, cols], preferred_element_type=F32)
        b_out[:, :, cols] = label_rows.astype(BF16).reshape(n, mb, wc)
    b_in[me] = b_out[me]

    others(lambda q: h_arrived(q).wait_recv())
    far_first(lambda q: b_copy(q).start())
    hidden = hg[...].reshape(tokens, width)

    pl_send[...] = jnp.dot(hidden, wt[...], preferred_element_type=F32)
    l_copy.start()
    others(lambda q: h_copy(q).wait_send())
    l_copy.wait_recv()
    logits = pl_send[...] + pl_recv[...]

    top = jnp.max(logits, axis=1, keepdims=True)
    exps = jnp.exp(logits - top)
    weights = jnp.where(hot, 0.0, exps).astype(BF16)

    def stats():
        total = jnp.sum(exps, axis=1, keepdims=True)
        aim = jnp.sum(jnp.where(hot, logits, 0.0), axis=1, keepdims=True)
        lanes = st.shape[2]
        diag = lax.broadcasted_iota(jnp.int32, (tokens, lanes), 1) == row_f

        def to_lanes(column):
            return jnp.sum(jnp.where(diag, column, 0.0), axis=0, keepdims=True)

        st[me] = jnp.concatenate(
            [to_lanes(top), to_lanes(total), to_lanes(aim), to_lanes(aim)], axis=0
        )
        far_first(lambda q: s_copy(q).start())

    def terms():
        step = min(1024, width)
        for c in range(width // step):
            cols = slice(c * step, (c + 1) * step)
            part = jnp.dot(weights, w[:, cols], preferred_element_type=F32)
            g_out[:, :, cols] = part.astype(BF16).reshape(n, mb, step)
        others(lambda q: g_copy(q).start())
        g_in[me] = g_out[me]

    stats()
    terms()

    l_copy.wait_send()
    others(lambda q: b_copy(q).wait_send())
    others(lambda q: s_copy(q).wait_send())

    others(lambda q: b_arrived(q).wait_recv())
    label_row = b_in[0].astype(F32)
    for d in range(1, n):
        label_row += b_in[d].astype(F32)

    others(lambda q: s_arrived(q).wait_recv())
    lanes = st.shape[2]
    lane = lax.broadcasted_iota(jnp.int32, (1, lanes), 1)
    spread = []
    pull = []
    for m in range(mb):
        mine = lane == me * mb + m

        def of_token(i):
            return jnp.sum(jnp.where(mine, st[:, i, :], 0.0), axis=1, keepdims=True)

        tops = of_token(0)
        row_max = jnp.max(tops, axis=0, keepdims=True)
        row_total = jnp.sum(of_token(1) * jnp.exp(tops - row_max), axis=0, keepdims=True)
        target = jnp.sum(of_token(2), axis=0, keepdims=True)
        log_total = row_max + jnp.log(row_total)
        loss_ref[:, m : m + 1] = log_total - target
        upstream = jnp.sum(
            jnp.where(
                lax.broadcasted_iota(jnp.int32, (1, n), 1) == me, up_ref[m : m + 1, :], 0.0
            ),
            axis=1,
            keepdims=True,
        )
        spread.append(upstream * jnp.exp(tops - log_total))
        pull.append(
            (upstream * (jnp.exp(target - log_total) - 1.0)).astype(BF16).astype(F32)
        )
    sums = jnp.concatenate(pull, axis=0) * label_row
    others(lambda q: g_copy(q).wait_send())
    others_back(lambda q: g_arrived(q).wait_recv())
    for d in range(n):
        scale = jnp.concatenate([spread[m][d : d + 1, :] for m in range(mb)], axis=0)
        sums += scale * g_in[d].astype(F32)
    grad_ref[...] = sums.astype(BF16)


def hand_over(loss_ref, grad_ref, loss_out, grad_out):
    loss_out[...] = loss_ref[...]
    grad_out[...] = grad_ref[...]


def on_device(n, hidden, labels, upstream, out_weight):
    mb, tok_dev, width = hidden.shape
    voc = out_weight.shape[0]
    tokens = n * mb
    chunks = 4
    lanes = -(-tokens // 128) * 128
    dma = pltpu.SemaphoreType.DMA
    vmem = pl.BlockSpec(memory_space=pltpu.VMEM)
    loss, grad = pl.pallas_call(
        functools.partial(kernel, n, mb, chunks),
        out_shape=(pltpu.VMEM((1, mb), F32), pltpu.VMEM((mb, width), BF16)),
        in_specs=[pl.BlockSpec(memory_space=pltpu.HBM)] * 4,
        out_specs=(vmem, vmem),
        scratch_shapes=[
            pltpu.VMEM((voc, width), BF16),
            pltpu.VMEM((width, voc), BF16),
            pltpu.VMEM((n, mb, width), BF16),
            pltpu.VMEM((tokens, voc), F32),
            pltpu.VMEM((tokens, voc), F32),
            pltpu.VMEM((n, 4, lanes), F32),
            pltpu.VMEM((n, mb, width), BF16),
            pltpu.VMEM((n, mb, width), BF16),
            pltpu.VMEM((n, mb, width), BF16),
            pltpu.VMEM((n, mb, width), BF16),
            pltpu.VMEM(labels.shape, labels.dtype),
            pltpu.VMEM(upstream.shape, upstream.dtype),
            dma((chunks,)),
            dma((3,)),
            dma((n,)),
            dma((n,)),
            dma,
            dma,
            dma((n,)),
            dma((n,)),
            dma((n,)),
            dma((n,)),
            dma((n,)),
            dma((n,)),
        ],
        compiler_params=pltpu.CompilerParams(
            collective_id=0, has_side_effects=True, vmem_limit_bytes=56 * 1024 * 1024
        ),
    )(hidden.reshape(mb, width), labels, upstream, out_weight)
    loss = pltpu.with_memory_space_constraint(loss, pltpu.VMEM)
    grad = pltpu.with_memory_space_constraint(grad, pltpu.VMEM)
    loss, grad = pl.pallas_call(
        hand_over,
        out_shape=(
            jax.ShapeDtypeStruct(loss.shape, loss.dtype),
            jax.ShapeDtypeStruct(grad.shape, grad.dtype),
        ),
        in_specs=[vmem, vmem],
        out_specs=(vmem, vmem),
    )(loss, grad)
    return loss.reshape(mb, tok_dev), grad.reshape(mb, tok_dev, width)


def solution(mesh):
    in_specs = (
        P(None, ("groups", "pipe"), "tensor"),
        P(None, "groups"),
        P(None, "groups"),
        P(("groups", "pipe"), "tensor"),
    )
    out_specs = (P(None, ("groups", "pipe")), P(None, ("groups", "pipe"), "tensor"))
    return jax.shard_map(
        functools.partial(on_device, mesh.shape["pipe"]),
        mesh=mesh,
        in_specs=in_specs,
        out_specs=out_specs,
        check_vma=False,
    )
```

```python
import functools

import jax
import jax.numpy as jnp
from jax import lax
from jax.experimental import pallas as pl
from jax.experimental.pallas import tpu as pltpu
from jax.sharding import PartitionSpec as P

F32 = jnp.float32
BF16 = jnp.bfloat16
UNROLL = 16


def each(count, body):
    if count <= UNROLL:
        for i in range(count):
            body(i)
    else:

        @pl.loop(0, count)
        def _(i):
            body(i)


def kernel(
    n,
    mb,
    chunks,
    h_hbm,
    lab_hbm,
    up_hbm,
    w_hbm,
    loss_ref,
    grad_ref,
    w,
    wt,
    hg,
    pl_send,
    pl_recv,
    st,
    b_out,
    b_in,
    g_out,
    g_in,
    lab_ref,
    up_ref,
    w_sem,
    in_sem,
    h_send,
    h_recv,
    l_send,
    l_recv,
    b_send,
    b_recv,
    s_send,
    s_recv,
    g_send,
    g_recv,
):
    me = lax.axis_index("pipe")
    core = lax.axis_index("tensor")
    voc, width = w_hbm.shape
    tokens = n * mb
    wc = width // chunks

    def other(i):
        return jnp.where(me <= i, i + 1, i)

    def others(body):
        each(n - 1, lambda i: body(other(i)))

    def far(i):
        return me ^ (n - 1 - i) if n & (n - 1) == 0 else lax.rem(me + 1 + i, n)

    def far_first(body, first=0, last=n - 1):
        each(last - first, lambda i: body(far(first + i)))

    def after_first(body):
        def one(i):
            @pl.when(me != i + 1)
            def _():
                body(i + 1)

        each(n - 1, one)

    def others_back(body):
        each(n - 1, lambda i: body(other(n - 2 - i)))

    barrier = pltpu.get_barrier_semaphore()
    others(lambda q: pl.semaphore_signal(barrier, inc=1, device_id={"pipe": q}))
    pl.semaphore_signal(barrier, inc=1, device_id={"tensor": 1 - core})

    def w_copy(c):
        part = pl.ds(c * wc, wc)
        return pltpu.make_async_copy(w_hbm.at[:, part], w.at[:, part], w_sem.at[c])

    inputs = (
        pltpu.make_async_copy(h_hbm, hg.at[me], in_sem.at[0]),
        pltpu.make_async_copy(lab_hbm, lab_ref, in_sem.at[1]),
        pltpu.make_async_copy(up_hbm, up_ref, in_sem.at[2]),
    )
    for copy in inputs:
        copy.start()
    inputs[0].wait()
    for c in range(chunks):
        w_copy(c).start()

    pl.semaphore_wait(barrier, n)

    def to_all(ref, send, recv):
        def copy(to):
            return pltpu.make_async_remote_copy(
                src_ref=ref.at[me],
                dst_ref=ref.at[me],
                send_sem=send.at[to],
                recv_sem=recv.at[me],
                device_id={"pipe": to},
            )

        def arrived(source):
            return pltpu.make_async_remote_copy(
                src_ref=ref.at[source],
                dst_ref=ref.at[source],
                send_sem=send.at[source],
                recv_sem=recv.at[source],
                device_id={"pipe": source},
            )

        return copy, arrived

    def to_owners(out, into, send, recv):
        def copy(to):
            return pltpu.make_async_remote_copy(
                src_ref=out.at[to],
                dst_ref=into.at[me],
                send_sem=send.at[to],
                recv_sem=recv.at[me],
                device_id={"pipe": to},
            )

        def arrived(source):
            return pltpu.make_async_remote_copy(
                src_ref=out.at[source],
                dst_ref=into.at[source],
                send_sem=send.at[source],
                recv_sem=recv.at[source],
                device_id={"pipe": source},
            )

        return copy, arrived

    h_copy, h_arrived = to_all(hg, h_send, h_recv)
    b_copy, b_arrived = to_owners(b_out, b_in, b_send, b_recv)
    s_copy, s_arrived = to_all(st, s_send, s_recv)
    g_copy, g_arrived = to_owners(g_out, g_in, g_send, g_recv)
    l_copy = pltpu.make_async_remote_copy(
        src_ref=pl_send,
        dst_ref=pl_recv,
        send_sem=l_send,
        recv_sem=l_recv,
        device_id={"tensor": 1 - core},
    )

    far_first(lambda q: h_copy(q).start())

    inputs[1].wait()
    inputs[2].wait()
    row_f = lax.broadcasted_iota(jnp.int32, (tokens, 1), 0)
    row_tok = row_f // mb
    row_mb = row_f - row_tok * mb
    tok_cols = lax.broadcasted_iota(jnp.int32, (tokens, n), 1)
    label_of = jnp.zeros((tokens, n), F32)
    for m in range(mb):
        label_of = jnp.where(
            (row_mb == m) & (row_tok == tok_cols), lab_ref[m : m + 1, :].astype(F32), label_of
        )
    labels = jnp.sum(label_of, axis=1, keepdims=True).astype(jnp.int32) - me * voc
    hot = labels == lax.broadcasted_iota(jnp.int32, (tokens, voc), 1)


    hot_rows = hot.astype(F32).astype(BF16)
    for c in range(chunks):
        w_copy(c).wait()
        cols = slice(c * wc, (c + 1) * wc)
        wt[cols, :] = w[:, cols].T
        label_rows = jnp.dot(hot_rows, w[:, cols], preferred_element_type=F32)
        b_out[:, :, cols] = label_rows.astype(BF16).reshape(n, mb, wc)
    b_in[me] = b_out[me]

    distant = n // 2
    far_first(lambda q: b_copy(q).start(), distant, n - 1)
    others(lambda q: h_arrived(q).wait_recv())
    far_first(lambda q: b_copy(q).start(), 0, distant)
    hidden = hg[...].reshape(tokens, width)

    pl_send[...] = jnp.dot(hidden, wt[...], preferred_element_type=F32)
    l_copy.start()
    l_copy.wait_recv()
    logits = pl_send[...] + pl_recv[...]

    top = jnp.max(logits, axis=1, keepdims=True)
    exps = jnp.exp(logits - top)
    weights = jnp.where(hot, 0.0, exps).astype(BF16)

    def stats():
        total = jnp.sum(exps, axis=1, keepdims=True)
        aim = jnp.sum(jnp.where(hot, logits, 0.0), axis=1, keepdims=True)
        lanes = st.shape[2]
        diag = lax.broadcasted_iota(jnp.int32, (tokens, lanes), 1) == row_f

        def to_lanes(column):
            return jnp.sum(jnp.where(diag, column, 0.0), axis=0, keepdims=True)

        st[me] = jnp.concatenate(
            [to_lanes(top), to_lanes(total), to_lanes(aim), to_lanes(aim)], axis=0
        )
        far_first(lambda q: s_copy(q).start())

    def terms():
        step = min(1024, width)
        for c in range(width // step):
            cols = slice(c * step, (c + 1) * step)
            part = jnp.dot(weights, w[:, cols], preferred_element_type=F32)
            g_out[:, :, cols] = part.astype(BF16).reshape(n, mb, step)
        def to_first(body):
            @pl.when(me != 0)
            def _():
                body(g_copy(0))

        to_first(lambda copy: copy.start())
        g_in[me] = g_out[me]
        to_first(lambda copy: copy.wait_send())
        after_first(lambda q: g_copy(q).start())

    stats()
    terms()

    others(lambda q: h_copy(q).wait_send())
    l_copy.wait_send()
    others(lambda q: b_copy(q).wait_send())
    others(lambda q: s_copy(q).wait_send())

    others(lambda q: b_arrived(q).wait_recv())
    label_row = b_in[0].astype(F32)
    for d in range(1, n):
        label_row += b_in[d].astype(F32)

    others(lambda q: s_arrived(q).wait_recv())
    lanes = st.shape[2]
    lane = lax.broadcasted_iota(jnp.int32, (1, lanes), 1)
    spread = []
    pull = []
    for m in range(mb):
        mine = lane == me * mb + m

        def of_token(i):
            return jnp.sum(jnp.where(mine, st[:, i, :], 0.0), axis=1, keepdims=True)

        tops = of_token(0)
        row_max = jnp.max(tops, axis=0, keepdims=True)
        row_total = jnp.sum(of_token(1) * jnp.exp(tops - row_max), axis=0, keepdims=True)
        target = jnp.sum(of_token(2), axis=0, keepdims=True)
        log_total = row_max + jnp.log(row_total)
        loss_ref[:, m : m + 1] = log_total - target
        upstream = jnp.sum(
            jnp.where(
                lax.broadcasted_iota(jnp.int32, (1, n), 1) == me, up_ref[m : m + 1, :], 0.0
            ),
            axis=1,
            keepdims=True,
        )
        spread.append(upstream * jnp.exp(tops - log_total))
        pull.append(
            (upstream * (jnp.exp(target - log_total) - 1.0)).astype(BF16).astype(F32)
        )
    sums = jnp.concatenate(pull, axis=0) * label_row
    after_first(lambda q: g_copy(q).wait_send())
    others_back(lambda q: g_arrived(q).wait_recv())
    for d in range(n):
        scale = jnp.concatenate([spread[m][d : d + 1, :] for m in range(mb)], axis=0)
        sums += scale * g_in[d].astype(F32)
    grad_ref[...] = sums.astype(BF16)


def hand_over(loss_ref, grad_ref, loss_out, grad_out):
    loss_out[...] = loss_ref[...]
    grad_out[...] = grad_ref[...]


def on_device(n, hidden, labels, upstream, out_weight):
    mb, tok_dev, width = hidden.shape
    voc = out_weight.shape[0]
    tokens = n * mb
    chunks = 4
    lanes = -(-tokens // 128) * 128
    dma = pltpu.SemaphoreType.DMA
    vmem = pl.BlockSpec(memory_space=pltpu.VMEM)
    loss, grad = pl.pallas_call(
        functools.partial(kernel, n, mb, chunks),
        out_shape=(pltpu.VMEM((1, mb), F32), pltpu.VMEM((mb, width), BF16)),
        in_specs=[pl.BlockSpec(memory_space=pltpu.HBM)] * 4,
        out_specs=(vmem, vmem),
        scratch_shapes=[
            pltpu.VMEM((voc, width), BF16),
            pltpu.VMEM((width, voc), BF16),
            pltpu.VMEM((n, mb, width), BF16),
            pltpu.VMEM((tokens, voc), F32),
            pltpu.VMEM((tokens, voc), F32),
            pltpu.VMEM((n, 4, lanes), F32),
            pltpu.VMEM((n, mb, width), BF16),
            pltpu.VMEM((n, mb, width), BF16),
            pltpu.VMEM((n, mb, width), BF16),
            pltpu.VMEM((n, mb, width), BF16),
            pltpu.VMEM(labels.shape, labels.dtype),
            pltpu.VMEM(upstream.shape, upstream.dtype),
            dma((chunks,)),
            dma((3,)),
            dma((n,)),
            dma((n,)),
            dma,
            dma,
            dma((n,)),
            dma((n,)),
            dma((n,)),
            dma((n,)),
            dma((n,)),
            dma((n,)),
        ],
        compiler_params=pltpu.CompilerParams(
            collective_id=0, has_side_effects=True, vmem_limit_bytes=56 * 1024 * 1024
        ),
    )(hidden.reshape(mb, width), labels, upstream, out_weight)
    loss = pltpu.with_memory_space_constraint(loss, pltpu.VMEM)
    grad = pltpu.with_memory_space_constraint(grad, pltpu.VMEM)
    loss, grad = pl.pallas_call(
        hand_over,
        out_shape=(
            jax.ShapeDtypeStruct(loss.shape, loss.dtype),
            jax.ShapeDtypeStruct(grad.shape, grad.dtype),
        ),
        in_specs=[vmem, vmem],
        out_specs=(vmem, vmem),
    )(loss, grad)
    return loss.reshape(mb, tok_dev), grad.reshape(mb, tok_dev, width)


def solution(mesh):
    in_specs = (
        P(None, ("groups", "pipe"), "tensor"),
        P(None, "groups"),
        P(None, "groups"),
        P(("groups", "pipe"), "tensor"),
    )
    out_specs = (P(None, ("groups", "pipe")), P(None, ("groups", "pipe"), "tensor"))
    return jax.shard_map(
        functools.partial(on_device, mesh.shape["pipe"]),
        mesh=mesh,
        in_specs=in_specs,
        out_specs=out_specs,
        check_vma=False,
    )
```

```python
import functools

import jax
import jax.numpy as jnp
from jax import lax
from jax.experimental import pallas as pl
from jax.experimental.pallas import tpu as pltpu
from jax.sharding import PartitionSpec as P

F32 = jnp.float32
BF16 = jnp.bfloat16
UNROLL = 16


def each(count, body):
    if count <= UNROLL:
        for i in range(count):
            body(i)
    else:

        @pl.loop(0, count)
        def _(i):
            body(i)


def kernel(
    n,
    mb,
    chunks,
    h_hbm,
    lab_hbm,
    up_hbm,
    w_hbm,
    loss_ref,
    grad_ref,
    w,
    wt,
    hg,
    pl_send,
    pl_recv,
    st,
    b_out,
    b_in,
    g_out,
    g_in,
    lab_ref,
    up_ref,
    w_sem,
    in_sem,
    h_send,
    h_recv,
    l_send,
    l_recv,
    b_send,
    b_recv,
    s_send,
    s_recv,
    g_send,
    g_recv,
):
    me = lax.axis_index("pipe")
    core = lax.axis_index("tensor")
    voc, width = w_hbm.shape
    tokens = n * mb
    wc = width // chunks

    def other(i):
        return jnp.where(me <= i, i + 1, i)

    def others(body):
        each(n - 1, lambda i: body(other(i)))

    def far(i):
        return me ^ (n - 1 - i) if n & (n - 1) == 0 else lax.rem(me + 1 + i, n)

    def far_first(body, first=0, last=n - 1):
        each(last - first, lambda i: body(far(first + i)))

    def after_first(body):
        def one(i):
            @pl.when(me != i + 1)
            def _():
                body(i + 1)

        each(n - 1, one)

    def others_back(body):
        each(n - 1, lambda i: body(other(n - 2 - i)))

    barrier = pltpu.get_barrier_semaphore()
    others(lambda q: pl.semaphore_signal(barrier, inc=1, device_id={"pipe": q}))
    pl.semaphore_signal(barrier, inc=1, device_id={"tensor": 1 - core})

    def w_copy(c):
        part = pl.ds(c * wc, wc)
        return pltpu.make_async_copy(w_hbm.at[:, part], w.at[:, part], w_sem.at[c])

    inputs = (
        pltpu.make_async_copy(h_hbm, hg.at[me], in_sem.at[0]),
        pltpu.make_async_copy(lab_hbm, lab_ref, in_sem.at[1]),
        pltpu.make_async_copy(up_hbm, up_ref, in_sem.at[2]),
    )
    for copy in inputs:
        copy.start()
    inputs[0].wait()
    for c in range(chunks):
        w_copy(c).start()

    pl.semaphore_wait(barrier, n)

    def to_all(ref, send, recv):
        def copy(to):
            return pltpu.make_async_remote_copy(
                src_ref=ref.at[me],
                dst_ref=ref.at[me],
                send_sem=send.at[to],
                recv_sem=recv.at[me],
                device_id={"pipe": to},
            )

        def arrived(source):
            return pltpu.make_async_remote_copy(
                src_ref=ref.at[source],
                dst_ref=ref.at[source],
                send_sem=send.at[source],
                recv_sem=recv.at[source],
                device_id={"pipe": source},
            )

        return copy, arrived

    def to_owners(out, into, send, recv):
        def copy(to):
            return pltpu.make_async_remote_copy(
                src_ref=out.at[to],
                dst_ref=into.at[me],
                send_sem=send.at[to],
                recv_sem=recv.at[me],
                device_id={"pipe": to},
            )

        def arrived(source):
            return pltpu.make_async_remote_copy(
                src_ref=out.at[source],
                dst_ref=into.at[source],
                send_sem=send.at[source],
                recv_sem=recv.at[source],
                device_id={"pipe": source},
            )

        return copy, arrived

    h_copy, h_arrived = to_all(hg, h_send, h_recv)
    b_copy, b_arrived = to_owners(b_out, b_in, b_send, b_recv)
    s_copy, s_arrived = to_all(st, s_send, s_recv)
    g_copy, g_arrived = to_owners(g_out, g_in, g_send, g_recv)
    l_copy = pltpu.make_async_remote_copy(
        src_ref=pl_send,
        dst_ref=pl_recv,
        send_sem=l_send,
        recv_sem=l_recv,
        device_id={"tensor": 1 - core},
    )

    far_first(lambda q: h_copy(q).start(), 0, n // 2)

    inputs[1].wait()
    inputs[2].wait()
    row_f = lax.broadcasted_iota(jnp.int32, (tokens, 1), 0)
    row_tok = row_f // mb
    row_mb = row_f - row_tok * mb
    tok_cols = lax.broadcasted_iota(jnp.int32, (tokens, n), 1)
    label_of = jnp.zeros((tokens, n), F32)
    for m in range(mb):
        label_of = jnp.where(
            (row_mb == m) & (row_tok == tok_cols), lab_ref[m : m + 1, :].astype(F32), label_of
        )
    labels = jnp.sum(label_of, axis=1, keepdims=True).astype(jnp.int32) - me * voc
    hot = labels == lax.broadcasted_iota(jnp.int32, (tokens, voc), 1)


    hot_rows = hot.astype(F32).astype(BF16)
    for c in range(chunks):
        w_copy(c).wait()
        if c == 0:
            far_first(lambda q: h_copy(q).start(), n // 2, n - 1)
        cols = slice(c * wc, (c + 1) * wc)
        wt[cols, :] = w[:, cols].T
        label_rows = jnp.dot(hot_rows, w[:, cols], preferred_element_type=F32)
        b_out[:, :, cols] = label_rows.astype(BF16).reshape(n, mb, wc)
    b_in[me] = b_out[me]

    distant = n // 2
    far_first(lambda q: b_copy(q).start(), distant, n - 1)
    others(lambda q: h_arrived(q).wait_recv())
    far_first(lambda q: b_copy(q).start(), 0, distant)
    hidden = hg[...].reshape(tokens, width)

    pl_send[...] = jnp.dot(hidden, wt[...], preferred_element_type=F32)
    l_copy.start()
    l_copy.wait_recv()
    logits = pl_send[...] + pl_recv[...]

    top = jnp.max(logits, axis=1, keepdims=True)
    exps = jnp.exp(logits - top)
    weights = jnp.where(hot, 0.0, exps).astype(BF16)

    def stats():
        total = jnp.sum(exps, axis=1, keepdims=True)
        aim = jnp.sum(jnp.where(hot, logits, 0.0), axis=1, keepdims=True)
        lanes = st.shape[2]
        diag = lax.broadcasted_iota(jnp.int32, (tokens, lanes), 1) == row_f

        def to_lanes(column):
            return jnp.sum(jnp.where(diag, column, 0.0), axis=0, keepdims=True)

        st[me] = jnp.concatenate(
            [to_lanes(top), to_lanes(total), to_lanes(aim), to_lanes(aim)], axis=0
        )
        far_first(lambda q: s_copy(q).start())

    def terms():
        step = min(1024, width)
        for c in range(width // step):
            cols = slice(c * step, (c + 1) * step)
            part = jnp.dot(weights, w[:, cols], preferred_element_type=F32)
            g_out[:, :, cols] = part.astype(BF16).reshape(n, mb, step)
        def to_first(body):
            @pl.when(me != 0)
            def _():
                body(g_copy(0))

        to_first(lambda copy: copy.start())
        g_in[me] = g_out[me]
        to_first(lambda copy: pl.when(core == 0)(lambda: copy.wait_send()))
        after_first(lambda q: g_copy(q).start())

    stats()
    terms()

    others(lambda q: h_copy(q).wait_send())
    l_copy.wait_send()
    others(lambda q: b_copy(q).wait_send())
    others(lambda q: s_copy(q).wait_send())

    others(lambda q: b_arrived(q).wait_recv())
    label_row = b_in[0].astype(F32)
    for d in range(1, n):
        label_row += b_in[d].astype(F32)

    others(lambda q: s_arrived(q).wait_recv())
    lanes = st.shape[2]
    lane = lax.broadcasted_iota(jnp.int32, (1, lanes), 1)
    spread = []
    pull = []
    for m in range(mb):
        mine = lane == me * mb + m

        def of_token(i):
            return jnp.sum(jnp.where(mine, st[:, i, :], 0.0), axis=1, keepdims=True)

        tops = of_token(0)
        row_max = jnp.max(tops, axis=0, keepdims=True)
        row_total = jnp.sum(of_token(1) * jnp.exp(tops - row_max), axis=0, keepdims=True)
        target = jnp.sum(of_token(2), axis=0, keepdims=True)
        log_total = row_max + jnp.log(row_total)
        loss_ref[:, m : m + 1] = log_total - target
        upstream = jnp.sum(
            jnp.where(
                lax.broadcasted_iota(jnp.int32, (1, n), 1) == me, up_ref[m : m + 1, :], 0.0
            ),
            axis=1,
            keepdims=True,
        )
        spread.append(upstream * jnp.exp(tops - log_total))
        pull.append(
            (upstream * (jnp.exp(target - log_total) - 1.0)).astype(BF16).astype(F32)
        )
    sums = jnp.concatenate(pull, axis=0) * label_row
    @pl.when((me != 0) & (core == 1))
    def _():
        g_copy(0).wait_send()

    after_first(lambda q: g_copy(q).wait_send())
    others_back(lambda q: g_arrived(q).wait_recv())
    for d in range(n):
        scale = jnp.concatenate([spread[m][d : d + 1, :] for m in range(mb)], axis=0)
        sums += scale * g_in[d].astype(F32)
    grad_ref[...] = sums.astype(BF16)


def hand_over(loss_ref, grad_ref, loss_out, grad_out):
    loss_out[...] = loss_ref[...]
    grad_out[...] = grad_ref[...]


def on_device(n, hidden, labels, upstream, out_weight):
    mb, tok_dev, width = hidden.shape
    voc = out_weight.shape[0]
    tokens = n * mb
    chunks = 4
    lanes = -(-tokens // 128) * 128
    dma = pltpu.SemaphoreType.DMA
    vmem = pl.BlockSpec(memory_space=pltpu.VMEM)
    loss, grad = pl.pallas_call(
        functools.partial(kernel, n, mb, chunks),
        out_shape=(pltpu.VMEM((1, mb), F32), pltpu.VMEM((mb, width), BF16)),
        in_specs=[pl.BlockSpec(memory_space=pltpu.HBM)] * 4,
        out_specs=(vmem, vmem),
        scratch_shapes=[
            pltpu.VMEM((voc, width), BF16),
            pltpu.VMEM((width, voc), BF16),
            pltpu.VMEM((n, mb, width), BF16),
            pltpu.VMEM((tokens, voc), F32),
            pltpu.VMEM((tokens, voc), F32),
            pltpu.VMEM((n, 4, lanes), F32),
            pltpu.VMEM((n, mb, width), BF16),
            pltpu.VMEM((n, mb, width), BF16),
            pltpu.VMEM((n, mb, width), BF16),
            pltpu.VMEM((n, mb, width), BF16),
            pltpu.VMEM(labels.shape, labels.dtype),
            pltpu.VMEM(upstream.shape, upstream.dtype),
            dma((chunks,)),
            dma((3,)),
            dma((n,)),
            dma((n,)),
            dma,
            dma,
            dma((n,)),
            dma((n,)),
            dma((n,)),
            dma((n,)),
            dma((n,)),
            dma((n,)),
        ],
        compiler_params=pltpu.CompilerParams(
            collective_id=0, has_side_effects=True, vmem_limit_bytes=56 * 1024 * 1024
        ),
    )(hidden.reshape(mb, width), labels, upstream, out_weight)
    loss = pltpu.with_memory_space_constraint(loss, pltpu.VMEM)
    grad = pltpu.with_memory_space_constraint(grad, pltpu.VMEM)
    loss, grad = pl.pallas_call(
        hand_over,
        out_shape=(
            jax.ShapeDtypeStruct(loss.shape, loss.dtype),
            jax.ShapeDtypeStruct(grad.shape, grad.dtype),
        ),
        in_specs=[vmem, vmem],
        out_specs=(vmem, vmem),
    )(loss, grad)
    return loss.reshape(mb, tok_dev), grad.reshape(mb, tok_dev, width)


def solution(mesh):
    in_specs = (
        P(None, ("groups", "pipe"), "tensor"),
        P(None, "groups"),
        P(None, "groups"),
        P(("groups", "pipe"), "tensor"),
    )
    out_specs = (P(None, ("groups", "pipe")), P(None, ("groups", "pipe"), "tensor"))
    return jax.shard_map(
        functools.partial(on_device, mesh.shape["pipe"]),
        mesh=mesh,
        in_specs=in_specs,
        out_specs=out_specs,
        check_vma=False,
    )
```

```python
import functools

import jax
import jax.numpy as jnp
from jax import lax
from jax.experimental import pallas as pl
from jax.experimental.pallas import tpu as pltpu
from jax.sharding import PartitionSpec as P

F32 = jnp.float32
BF16 = jnp.bfloat16
UNROLL = 16


def each(count, body):
    if count <= UNROLL:
        for i in range(count):
            body(i)
    else:

        @pl.loop(0, count)
        def _(i):
            body(i)


def kernel(
    n,
    mb,
    chunks,
    h_hbm,
    lab_hbm,
    up_hbm,
    w_hbm,
    loss_ref,
    grad_ref,
    w,
    wt,
    hg,
    pl_send,
    pl_recv,
    st,
    b_out,
    b_in,
    g_out,
    g_in,
    lab_ref,
    up_ref,
    w_sem,
    in_sem,
    h_send,
    h_recv,
    l_send,
    l_recv,
    b_send,
    b_recv,
    s_send,
    s_recv,
    g_send,
    g_recv,
):
    me = lax.axis_index("pipe")
    core = lax.axis_index("tensor")
    voc, width = w_hbm.shape
    tokens = n * mb
    wc = width // chunks

    def other(i):
        return jnp.where(me <= i, i + 1, i)

    def others(body):
        each(n - 1, lambda i: body(other(i)))

    def far(i):
        return me ^ (n - 1 - i) if n & (n - 1) == 0 else lax.rem(me + 1 + i, n)

    def far_first(body, first=0, last=n - 1):
        each(last - first, lambda i: body(far(first + i)))

    def after_first(body):
        def one(i):
            @pl.when(me != i + 1)
            def _():
                body(i + 1)

        each(n - 1, one)

    def others_back(body):
        each(n - 1, lambda i: body(other(n - 2 - i)))

    barrier = pltpu.get_barrier_semaphore()
    others(lambda q: pl.semaphore_signal(barrier, inc=1, device_id={"pipe": q}))
    pl.semaphore_signal(barrier, inc=1, device_id={"tensor": 1 - core})

    def w_copy(c):
        part = pl.ds(c * wc, wc)
        return pltpu.make_async_copy(w_hbm.at[:, part], w.at[:, part], w_sem.at[c])

    inputs = (
        pltpu.make_async_copy(h_hbm, hg.at[me], in_sem.at[0]),
        pltpu.make_async_copy(lab_hbm, lab_ref, in_sem.at[1]),
        pltpu.make_async_copy(up_hbm, up_ref, in_sem.at[2]),
    )
    for copy in inputs:
        copy.start()
    inputs[0].wait()
    for c in range(chunks):
        w_copy(c).start()

    pl.semaphore_wait(barrier, n)

    def to_all(ref, send, recv):
        def copy(to):
            return pltpu.make_async_remote_copy(
                src_ref=ref.at[me],
                dst_ref=ref.at[me],
                send_sem=send.at[to],
                recv_sem=recv.at[me],
                device_id={"pipe": to},
            )

        def arrived(source):
            return pltpu.make_async_remote_copy(
                src_ref=ref.at[source],
                dst_ref=ref.at[source],
                send_sem=send.at[source],
                recv_sem=recv.at[source],
                device_id={"pipe": source},
            )

        return copy, arrived

    def to_owners(out, into, send, recv):
        def copy(to):
            return pltpu.make_async_remote_copy(
                src_ref=out.at[to],
                dst_ref=into.at[me],
                send_sem=send.at[to],
                recv_sem=recv.at[me],
                device_id={"pipe": to},
            )

        def arrived(source):
            return pltpu.make_async_remote_copy(
                src_ref=out.at[source],
                dst_ref=into.at[source],
                send_sem=send.at[source],
                recv_sem=recv.at[source],
                device_id={"pipe": source},
            )

        return copy, arrived

    h_copy, h_arrived = to_all(hg, h_send, h_recv)
    b_copy, b_arrived = to_owners(b_out, b_in, b_send, b_recv)
    s_copy, s_arrived = to_all(st, s_send, s_recv)
    g_copy, g_arrived = to_owners(g_out, g_in, g_send, g_recv)
    l_copy = pltpu.make_async_remote_copy(
        src_ref=pl_send,
        dst_ref=pl_recv,
        send_sem=l_send,
        recv_sem=l_recv,
        device_id={"tensor": 1 - core},
    )

    far_first(lambda q: h_copy(q).start(), 0, n // 2)

    inputs[1].wait()
    inputs[2].wait()
    row_f = lax.broadcasted_iota(jnp.int32, (tokens, 1), 0)
    row_tok = row_f // mb
    row_mb = row_f - row_tok * mb
    tok_cols = lax.broadcasted_iota(jnp.int32, (tokens, n), 1)
    label_of = jnp.zeros((tokens, n), F32)
    for m in range(mb):
        label_of = jnp.where(
            (row_mb == m) & (row_tok == tok_cols), lab_ref[m : m + 1, :].astype(F32), label_of
        )
    labels = jnp.sum(label_of, axis=1, keepdims=True).astype(jnp.int32) - me * voc
    hot = labels == lax.broadcasted_iota(jnp.int32, (tokens, voc), 1)


    hot_rows = hot.astype(F32).astype(BF16)
    for c in range(chunks):
        w_copy(c).wait()
        if c == 0:
            far_first(lambda q: h_copy(q).start(), n // 2, n - 1)
        cols = slice(c * wc, (c + 1) * wc)
        wt[cols, :] = w[:, cols].T
        label_rows = jnp.dot(hot_rows, w[:, cols], preferred_element_type=F32)
        b_out[:, :, cols] = label_rows.astype(BF16).reshape(n, mb, wc)
    b_in[me] = b_out[me]

    distant = n // 2
    far_first(lambda q: b_copy(q).start(), distant, n - 1)
    others(lambda q: h_arrived(q).wait_recv())
    far_first(lambda q: b_copy(q).start(), 0, distant)
    hidden = hg[...].reshape(tokens, width)

    pl_send[...] = jnp.dot(hidden, wt[...], preferred_element_type=F32)
    l_copy.start()
    l_copy.wait_recv()
    logits = pl_send[...] + pl_recv[...]

    top = jnp.max(logits, axis=1, keepdims=True)
    exps = jnp.exp(logits - top)
    weights = jnp.where(hot, 0.0, exps).astype(BF16)

    def stats():
        total = jnp.sum(exps, axis=1, keepdims=True)
        aim = jnp.sum(jnp.where(hot, logits, 0.0), axis=1, keepdims=True)
        lanes = st.shape[2]
        diag = lax.broadcasted_iota(jnp.int32, (tokens, lanes), 1) == row_f

        def to_lanes(column):
            return jnp.sum(jnp.where(diag, column, 0.0), axis=0, keepdims=True)

        st[me] = jnp.concatenate(
            [to_lanes(top), to_lanes(total), to_lanes(aim), to_lanes(aim)], axis=0
        )
        far_first(lambda q: s_copy(q).start())

    def terms():
        step = min(1024, width)
        for c in range(width // step):
            cols = slice(c * step, (c + 1) * step)
            part = jnp.dot(weights, w[:, cols], preferred_element_type=F32)
            g_out[:, :, cols] = part.astype(BF16).reshape(n, mb, step)
        def to_first(body):
            @pl.when(me != 0)
            def _():
                body(g_copy(0))

        to_first(lambda copy: copy.start())
        g_in[me] = g_out[me]
        to_first(lambda copy: pl.when(core == 0)(lambda: copy.wait_send()))
        after_first(lambda q: g_copy(q).start())

    stats()
    terms()

    others(lambda q: h_copy(q).wait_send())
    l_copy.wait_send()
    others(lambda q: b_copy(q).wait_send())
    others(lambda q: s_copy(q).wait_send())

    others(lambda q: b_arrived(q).wait_recv())
    label_row = b_in[0].astype(F32)
    for d in range(1, n):
        label_row += b_in[d].astype(F32)

    others(lambda q: s_arrived(q).wait_recv())
    lanes = st.shape[2]
    lane = lax.broadcasted_iota(jnp.int32, (1, lanes), 1)
    spread = []
    pull = []
    for m in range(mb):
        mine = lane == me * mb + m

        def of_token(i):
            return jnp.sum(jnp.where(mine, st[:, i, :], 0.0), axis=1, keepdims=True)

        tops = of_token(0)
        row_max = jnp.max(tops, axis=0, keepdims=True)
        row_total = jnp.sum(of_token(1) * jnp.exp(tops - row_max), axis=0, keepdims=True)
        target = jnp.sum(of_token(2), axis=0, keepdims=True)
        log_total = row_max + jnp.log(row_total)
        loss_ref[:, m : m + 1] = log_total - target
        upstream = jnp.sum(
            jnp.where(
                lax.broadcasted_iota(jnp.int32, (1, n), 1) == me, up_ref[m : m + 1, :], 0.0
            ),
            axis=1,
            keepdims=True,
        )
        spread.append(upstream * jnp.exp(tops - log_total))
        pull.append(
            (upstream * (jnp.exp(target - log_total) - 1.0)).astype(BF16).astype(F32)
        )
    sums = jnp.concatenate(pull, axis=0) * label_row
    @pl.when((me != 0) & (core == 1))
    def _():
        g_copy(0).wait_send()

    after_first(lambda q: g_copy(q).wait_send())
    def wait_for(e):
        @pl.when(me != e)
        def _():
            g_arrived(e).wait_recv()

    for d in range(n):
        if d == 0:
            each(n // 2, wait_for)
        if d == n // 2:
            each(n - n // 2, lambda i: wait_for(n // 2 + i))
        scale = jnp.concatenate([spread[m][d : d + 1, :] for m in range(mb)], axis=0)
        sums += scale * g_in[d].astype(F32)
    grad_ref[...] = sums.astype(BF16)


def hand_over(loss_ref, grad_ref, loss_out, grad_out):
    loss_out[...] = loss_ref[...]
    grad_out[...] = grad_ref[...]


def on_device(n, hidden, labels, upstream, out_weight):
    mb, tok_dev, width = hidden.shape
    voc = out_weight.shape[0]
    tokens = n * mb
    chunks = 4
    lanes = -(-tokens // 128) * 128
    dma = pltpu.SemaphoreType.DMA
    vmem = pl.BlockSpec(memory_space=pltpu.VMEM)
    loss, grad = pl.pallas_call(
        functools.partial(kernel, n, mb, chunks),
        out_shape=(pltpu.VMEM((1, mb), F32), pltpu.VMEM((mb, width), BF16)),
        in_specs=[pl.BlockSpec(memory_space=pltpu.HBM)] * 4,
        out_specs=(vmem, vmem),
        scratch_shapes=[
            pltpu.VMEM((voc, width), BF16),
            pltpu.VMEM((width, voc), BF16),
            pltpu.VMEM((n, mb, width), BF16),
            pltpu.VMEM((tokens, voc), F32),
            pltpu.VMEM((tokens, voc), F32),
            pltpu.VMEM((n, 4, lanes), F32),
            pltpu.VMEM((n, mb, width), BF16),
            pltpu.VMEM((n, mb, width), BF16),
            pltpu.VMEM((n, mb, width), BF16),
            pltpu.VMEM((n, mb, width), BF16),
            pltpu.VMEM(labels.shape, labels.dtype),
            pltpu.VMEM(upstream.shape, upstream.dtype),
            dma((chunks,)),
            dma((3,)),
            dma((n,)),
            dma((n,)),
            dma,
            dma,
            dma((n,)),
            dma((n,)),
            dma((n,)),
            dma((n,)),
            dma((n,)),
            dma((n,)),
        ],
        compiler_params=pltpu.CompilerParams(
            collective_id=0, has_side_effects=True, vmem_limit_bytes=56 * 1024 * 1024
        ),
    )(hidden.reshape(mb, width), labels, upstream, out_weight)
    loss = pltpu.with_memory_space_constraint(loss, pltpu.VMEM)
    grad = pltpu.with_memory_space_constraint(grad, pltpu.VMEM)
    loss, grad = pl.pallas_call(
        hand_over,
        out_shape=(
            jax.ShapeDtypeStruct(loss.shape, loss.dtype),
            jax.ShapeDtypeStruct(grad.shape, grad.dtype),
        ),
        in_specs=[vmem, vmem],
        out_specs=(vmem, vmem),
    )(loss, grad)
    return loss.reshape(mb, tok_dev), grad.reshape(mb, tok_dev, width)


def solution(mesh):
    in_specs = (
        P(None, ("groups", "pipe"), "tensor"),
        P(None, "groups"),
        P(None, "groups"),
        P(("groups", "pipe"), "tensor"),
    )
    out_specs = (P(None, ("groups", "pipe")), P(None, ("groups", "pipe"), "tensor"))
    return jax.shard_map(
        functools.partial(on_device, mesh.shape["pipe"]),
        mesh=mesh,
        in_specs=in_specs,
        out_specs=out_specs,
        check_vma=False,
    )
```
